128 devices in a mesh: seq: 16 (over y_lo, x, core), cb: 8 (over y_hi, z).
Axes of the slice: x: 4, y: 4 (y_hi: 2, y_lo: 2; y = y_hi * 2 + y_lo), z: 4, core: 2. Of those that a mesh axis runs over, the one named last changes fastest.
Arguments:
- hidden: bfloat16 [2, 2048, 4096], P(None, 'seq'), may hold values from -6 to 6
- temporal_gain: float32 [4096], replicated, may hold values from 0.5 to 2
- temporal_qkv: bfloat16 [3, 4096, 2048], P(None, None, 'cb'), may hold values from -10 to 10
- temporal_out: bfloat16 [2048, 4096], P('cb'), may hold values from -0.125 to 0.125
- codebook_ids: int32 [2, 2048, 8], P(None, 'seq', 'cb'), may hold values from 0 to 2047
- embedding: bfloat16 [8, 2048, 1024], P('cb'), may hold values from -6 to 6
- input_weight: bfloat16 [8, 4096, 1024], P('cb', 'seq'), may hold values from -0.09375 to 0.09375
- depth_gain: float32 [8, 1024], P('cb'), may hold values from 0.5 to 2
- depth_qkv: bfloat16 [8, 3, 1024, 1024], P('cb'), may hold values from -10 to 10
- depth_out: bfloat16 [8, 1024, 1024], P('cb'), may hold values from -0.1875 to 0.1875
Outputs:
- temporal: bfloat16 [2, 2048, 4096], P(None, 'seq')
- depth: bfloat16 [2, 2048, 8, 1024], P(None, 'seq', 'cb')
The draws below stay inside these ranges and needn't reach their ends.
All inputs are finite; a program needn't handle non-finite values.
Results may differ from the reference program's by a relative error of at most 0.017.
Values may be sent and summed in bfloat16 or wider, within the bound.
A program may use at most 128 MiB of HBM per device.

```python
import math
import jax
import jax.numpy as jnp
import numpy as np
from jax import lax

D = 4096
HEADS = 16
HD = 128
DW = 1024
DH = 16
DHD = 64
VOCAB = 2048
SEQS = 2
LEN = 2048
CODEBOOKS = 8
N_CB = 8


def shared_projection(key, width, head_count, head_size):
    first = jax.random.fold_in(key, 0)
    base = jnp.clip(jax.random.normal(first, (3, width, head_count * head_size), jnp.float32), -6.0, 6.0) / jnp.sqrt(jnp.float32(width))
    return base


def draw_temporal_qkv(key, part):
    return shared_projection(jax.random.fold_in(key, 11), D, HEADS, HD).astype(jnp.bfloat16)


def draw_depth_qkv(key, part):
    books = jax.random.split(jax.random.fold_in(key, 23), CODEBOOKS)
    stacked = jax.vmap(lambda book_key: shared_projection(book_key, DW, DH, DHD))(books)
    return stacked.astype(jnp.bfloat16)


def touch_ends(values, stream_key, least, largest):
    index_at = [jax.random.randint(jax.random.fold_in(stream_key, axis), (), 0, length) for axis, length in enumerate(values.shape)]
    widest = values.shape.index(max(values.shape))
    next_to = index_at[:widest] + [(index_at[widest] + 1) % values.shape[widest]] + index_at[widest + 1:]
    return values.at[tuple(index_at)].set(least).at[tuple(next_to)].set(largest)


def level_of(key, dims, cuts, smallest, high):
    loudness, own = 1.0, jax.random.fold_in(key, 6)
    for position, shards_of in cuts:
        steps = jnp.exp(jax.random.uniform(jax.random.fold_in(own, position), (shards_of,), jnp.float32, smallest / len(cuts), high / len(cuts)))
        loudness = loudness * jnp.repeat(steps, dims[position] // shards_of).reshape([-1 if axis == position else 1 for axis in range(len(dims))])
    return loudness


def rank_table(count, skew):
    loads = [(1 << 20) // math.isqrt(grade ** skew) + 1 for grade in range(1, count + 1)]
    deviation = 1 + sum(loads) // (1 << 30)
    return np.cumsum(np.array([max(1, weight // deviation) for weight in loads]))


def skewed_ids(own_key, dims, number_of, slope):
    table = rank_table(number_of, slope)
    ticket = jax.random.randint(jax.random.fold_in(own_key, 1), dims, 0, int(table[number_of - 1]))
    standing = jnp.searchsorted(jnp.asarray(table, jnp.int32), ticket, side="right")
    return jax.random.permutation(jax.random.fold_in(own_key, 2), number_of)[standing].astype(jnp.int32)


def normal_values(key, extent, deviation, bound, shards=(), kind=jnp.bfloat16):
    drawn = jax.random.normal(key, extent, jnp.float32) * deviation
    if len(shards) > 0:
        drawn = level_of(key, extent, shards, -0.22, 0.18) * drawn
    return jnp.clip(drawn, min=-bound, max=bound).astype(kind)


def setup_inputs(seed: int = 0) -> dict:
    key_list = jax.random.split(jax.random.key(seed), 11)
    return {
        "hidden": normal_values(key_list[0], (SEQS, LEN, D), 1.0, 6.0, ((1, 16),)),
        "temporal_gain": jnp.clip(jnp.exp(jax.random.uniform(key_list[1], (D,), jnp.float32, math.log(0.5), math.log(2.0))), 0.5, 2.0),
        "temporal_qkv": draw_temporal_qkv(jax.random.fold_in(key_list[10], 71), 0),
        "temporal_out": normal_values(key_list[3], (HEADS * HD, D), (HEADS * HD) ** -0.5, 0.125, ((0, 8),)),
        "codebook_ids": touch_ends(skewed_ids(key_list[4], (SEQS, LEN, CODEBOOKS), VOCAB, 2), jax.random.fold_in(key_list[4], 3), 0, VOCAB - 1).astype(jnp.int32),
        "embedding": normal_values(key_list[5], (CODEBOOKS, VOCAB, DW), 1.0, 6.0, ((0, 8),)),
        "input_weight": normal_values(key_list[6], (CODEBOOKS, D, DW), D ** -0.5, 0.09375, ((0, 8), (1, 16))),
        "depth_gain": jnp.clip(jnp.exp(math.log(2.0) - 1.3862944 * jax.random.uniform(key_list[7], (CODEBOOKS, DW), jnp.float32) ** level_of(key_list[7], (CODEBOOKS, DW), ((0, 8),), -0.2, 0.2)), 0.5, 2.0),
        "depth_qkv": draw_depth_qkv(jax.random.fold_in(key_list[10], 71), 0),
        "depth_out": normal_values(key_list[9], (CODEBOOKS, DW, DW), DW ** -0.5, 0.1875, ((0, 8),)),
    }


def normalize(values, scale):
    mean_sq = lax.optimization_barrier(jnp.mean(values * values, axis=-1, keepdims=True))
    return values * lax.rsqrt(mean_sq + 1e-05) * scale

def rounded(values):
    return lax.optimization_barrier(values.astype(jnp.bfloat16)).astype(jnp.float32)

def reference(hidden, temporal_gain, temporal_qkv, temporal_out, codebook_ids, embedding, input_weight, depth_gain, depth_qkv, depth_out):
    row_count = SEQS * LEN
    hidden_f = hidden.astype(jnp.float32)
    normed = normalize(hidden_f, temporal_gain).astype(jnp.bfloat16).reshape(row_count, D)
    projected = []
    for which in range(3):
        part_rows = jnp.dot(normed, temporal_qkv[which], preferred_element_type=jnp.float32).astype(jnp.bfloat16)
        projected.append(part_rows.reshape(SEQS, LEN, HEADS, HD).transpose(2, 0, 1, 3))
    positions = jnp.arange(LEN, dtype=jnp.int32)
    allowed = positions[:, None] >= positions[None, :]

    def one_head(operands):
        head_query, head_key, head_value = operands
        scores = jnp.einsum('sqd,skd->sqk', head_query.astype(jnp.float32), head_key.astype(jnp.float32)) / jnp.sqrt(jnp.float32(HD))
        scores = jnp.where(allowed[None], scores, -1e+30)
        highest = lax.optimization_barrier(jnp.max(scores, axis=-1, keepdims=True))
        weights = jnp.where(allowed[None], jnp.exp(scores - highest), 0.0)
        totals = lax.optimization_barrier(jnp.sum(weights, axis=-1, keepdims=True))
        mixed = jnp.einsum('sqk,skd->sqd', rounded(weights), head_value.astype(jnp.float32)) / totals
        return mixed.astype(jnp.bfloat16)
    mixed = lax.map(one_head, (projected[0], projected[1], projected[2]))
    mixed = mixed.transpose(1, 2, 0, 3).reshape(row_count, HEADS * HD)
    group_cols = HEADS * HD // N_CB
    summed = jnp.zeros((row_count, D), jnp.float32)
    for group_at in range(N_CB):
        term = jnp.dot(mixed[:, group_at * group_cols:(group_at + 1) * group_cols], temporal_out[group_at * group_cols:(group_at + 1) * group_cols], preferred_element_type=jnp.float32)
        summed = summed + rounded(term)
    temporal = (hidden_f.reshape(row_count, D) + summed).astype(jnp.bfloat16)
    id_rows = codebook_ids.reshape(row_count, CODEBOOKS).transpose(1, 0)

    def prepare(operands):
        in_weight, table, gain_row, qkv_weight, id_row = operands
        entry = jnp.take(table, id_row, axis=0).astype(jnp.float32)
        stream = (jnp.dot(temporal, in_weight, preferred_element_type=jnp.float32) + entry).astype(jnp.bfloat16)
        depth_normed = normalize(stream.astype(jnp.float32), gain_row).astype(jnp.bfloat16)
        book_query = jnp.dot(depth_normed, qkv_weight[0], preferred_element_type=jnp.float32).astype(jnp.bfloat16)
        book_key = jnp.dot(depth_normed, qkv_weight[1], preferred_element_type=jnp.float32).astype(jnp.bfloat16)
        book_value = jnp.dot(depth_normed, qkv_weight[2], preferred_element_type=jnp.float32).astype(jnp.bfloat16)
        return (stream, book_query, book_key, book_value)
    streams, queries, key_all, value_all = lax.map(prepare, (input_weight, embedding, depth_gain, depth_qkv, id_rows))
    key_heads = key_all.reshape(CODEBOOKS, row_count, DH, DHD)
    value_heads = value_all.reshape(CODEBOOKS, row_count, DH, DHD)
    book_numbers = jnp.arange(CODEBOOKS, dtype=jnp.int32)

    def attend(operands):
        book, query_rows, out_weight, stream_rows = operands
        query_heads = query_rows.reshape(row_count, DH, DHD).astype(jnp.float32)
        scores = jnp.einsum('rhd,jrhd->rhj', query_heads, key_heads.astype(jnp.float32)) / jnp.sqrt(jnp.float32(DHD))
        permitted = (book_numbers <= book)[None, None, :]
        scores = jnp.where(permitted, scores, -1e+30)
        highest = lax.optimization_barrier(jnp.max(scores, axis=-1, keepdims=True))
        weights = jnp.where(permitted, jnp.exp(scores - highest), 0.0)
        totals = lax.optimization_barrier(jnp.sum(weights, axis=-1))[..., None]
        book_mixed = jnp.einsum('rhj,jrhd->rhd', rounded(weights), value_heads.astype(jnp.float32)) / totals
        book_mixed = book_mixed.astype(jnp.bfloat16).reshape(row_count, DW)
        return (jnp.dot(book_mixed, out_weight, preferred_element_type=jnp.float32) + stream_rows.astype(jnp.float32)).astype(jnp.bfloat16)
    depth = lax.map(attend, (book_numbers, queries, depth_out, streams))
    depth = depth.transpose(1, 0, 2).reshape(SEQS, LEN, CODEBOOKS, DW)
    return (temporal.reshape(SEQS, LEN, D), depth)
```

```python
import jax
import jax.numpy as jnp
from jax import lax
from jax.experimental import pallas as pl
from jax.experimental.pallas import tpu as pltpu
from jax.sharding import PartitionSpec as P

MESH = pl.DeviceIdType.MESH
F32, BF16 = jnp.float32, jnp.bfloat16
EPS = 1e-05
CB_STEPS = [(0, 1), (0, 3), (0, 2), (1, 0), (1, 1), (1, 3), (1, 2)]
SEQ_STEPS = [(0, 1), (0, 3), (1, 0), (0, 2), (1, 1), (1, 3), (1, 2)]


def dot(a, b):
    return jnp.dot(a, b, preferred_element_type=F32)


def body(
    hidden, gain, qkv_w, out_w, ids, embedding, in_w, depth_gain, depth_qkv, depth_out,
    temporal_out, depth_res,
    hid, normed, wq, kvq, kv, qs, att, mix, wo, tb, win, emb, dw, do, acc, stream, dnorm, dsend, drecv, bsend, brecv,
    local_sem, kv_send, kv_recv, kvf_send, kvf_recv, q_send, q_recv, r_send, r_recv, m_send, m_recv,
    wo_send, wo_recv, t_send, t_recv, to_sem, wi_send, wi_recv, wf_send, wf_recv, d_send, d_recv, b_send, b_recv,
):
    s = lax.axis_index("seq")
    c = lax.axis_index("cb")
    yl, x, co = s // 8, (s // 2) % 4, s % 2
    yh, z = c // 4, c % 4
    rank = yl * 2 + co

    def cb_at(step, sign=1):
        return ((yh + step[0]) % 2) * 4 + (z + sign * step[1] + 4) % 4

    def seq_at(step, sign=1):
        return ((yl + step[0]) % 2) * 8 + ((x + sign * step[1] + 4) % 4) * 2 + co

    sibling = s + 1 - 2 * co

    def remote(src, dst, send, recv, device):
        return pltpu.make_async_remote_copy(
            src_ref=src, dst_ref=dst, send_sem=send, recv_sem=recv, device_id=device, device_id_type=MESH
        )

    def arrive(ref, sem):
        pltpu.make_async_copy(ref, ref, sem).wait()

    pending = []

    def send(copy, when=None):
        if when is None:
            copy.start()
        else:
            pl.when(when)(copy.start)
        pending.append((copy, when))

    barrier = pltpu.get_barrier_semaphore()
    for step in CB_STEPS:
        pl.semaphore_signal(barrier, inc=1, device_id=(s, cb_at(step)), device_id_type=MESH)
    for step in SEQ_STEPS:
        pl.semaphore_signal(barrier, inc=1, device_id=(seq_at(step), c), device_id_type=MESH)
        other = seq_at(step) + 1 - 2 * co
        pl.semaphore_signal(barrier, inc=1, device_id=(other, c), device_id_type=MESH)
    pl.semaphore_signal(barrier, inc=1, device_id=(sibling, c), device_id_type=MESH)

    loads = [
        pltpu.make_async_copy(hidden, hid, local_sem.at[0]),
        pltpu.make_async_copy(qkv_w.at[1], wq.at[1], local_sem.at[1]),
        pltpu.make_async_copy(qkv_w.at[2], wq.at[2], local_sem.at[2]),
        pltpu.make_async_copy(qkv_w.at[0], wq.at[0], local_sem.at[3]),
        pltpu.make_async_copy(out_w.at[:, pl.ds(pl.multiple_of(c * 512, 512), 512)], wo.at[c], local_sem.at[4]),
        pltpu.make_async_copy(in_w, win.at[s], local_sem.at[5]),
        pltpu.make_async_copy(embedding, emb, local_sem.at[6]),
        pltpu.make_async_copy(depth_qkv, dw, local_sem.at[7]),
        pltpu.make_async_copy(depth_out, do, local_sem.at[8]),
    ]
    for copy in loads:
        copy.start()

    loads[0].wait()

    @pl.loop(0, 16)
    def _(i):
        rows = pl.ds(pl.multiple_of(i * 16, 16), 16)
        values = hid[rows, :].astype(F32)
        mean_sq = jnp.mean(values * values, axis=-1, keepdims=True)
        normed[rows, :] = (values * lax.rsqrt(mean_sq + EPS) * gain[...]).astype(BF16)

    def project(which, slot):
        loads[{1: 1, 2: 2, 0: 3}[which]].wait()
        res = dot(normed[...], wq[which]).astype(BF16)
        for g in range(4):
            b, h = g // 2, g % 2
            kvq[g, slot] = res[b * 128 : (b + 1) * 128, h * 128 : (h + 1) * 128]

    project(1, 0)
    project(2, 1)
    pl.semaphore_wait(barrier, 22)

    for i, step in enumerate(SEQ_STEPS):
        to = seq_at(step)
        g = (to // 2) % 4
        send(remote(kvq.at[g, pl.ds(0, 2)], kv.at[s], kv_send.at[i], kv_recv.at[i], (to, c)))
    kv[s] = kvq[x, 0:2]
    send(remote(kv.at[s], kv.at[s], kvf_send.at[7], kvf_recv.at[7], (sibling, c)))

    for i, step in enumerate(CB_STEPS):
        to = cb_at(step)
        columns = pl.ds(pl.multiple_of(to * 512, 512), 512)
        send(remote(out_w.at[:, columns], wo.at[c], wo_send.at[i], wo_recv.at[i], (s, to)))

    project(0, 2)
    turn = s % 8
    owner = jnp.where(turn < 4, turn, 7 - turn)
    strip = s // 4
    for dx in range(4):
        g = (x + dx) % 4
        to = (owner // 2) * 8 + g * 2 + owner % 2
        copy = remote(kvq.at[g, 2], qs.at[strip], q_send.at[dx], q_recv.at[strip], (to, c))
        send(copy, None if dx else owner != rank)

    @pl.when(owner == rank)
    def _():
        qs[strip] = kvq[x, 2]

    send(remote(in_w, win.at[s], wi_send.at[0], wi_recv.at[0], (seq_at((1, 0)), c)))
    for i in (1, 3, 2):
        send(remote(in_w, win.at[s], wi_send.at[i], wi_recv.at[i], (seq_at((0, i)), c)))
    send(remote(in_w, win.at[s], wf_send.at[0], wf_recv.at[0], (sibling, c)))

    for i, step in enumerate(SEQ_STEPS):
        source = seq_at(step, -1)
        arrive(kv.at[source], kv_recv.at[i])
        send(remote(kv.at[source], kv.at[source], kvf_send.at[i], kvf_recv.at[i], (sibling, c)))
    arrive(kv.at[sibling], kvf_recv.at[7])
    for i, step in enumerate(SEQ_STEPS):
        source = seq_at(step, -1) + 1 - 2 * co
        arrive(kv.at[source], kvf_recv.at[i])

    for k in range(4):
        block = 4 * k + (rank if k % 2 == 0 else 3 - rank)

        @pl.when(block != s)
        def _():
            arrive(qs.at[k], q_recv.at[k])

        n = 4 * (k + 1)
        keys = kv[0:n, 0].reshape(n * 128, 128)
        values = kv[0:n, 1].reshape(n * 128, 128)
        scores = lax.dot_general(qs[k], keys, (((1,), (1,)), ((), ())), preferred_element_type=F32)
        row = lax.broadcasted_iota(jnp.int32, scores.shape, 0) + block * 128
        col = lax.broadcasted_iota(jnp.int32, scores.shape, 1)
        allowed = col <= row
        scores = jnp.where(allowed, scores * (128.0**-0.5), -1e30)
        weights = jnp.where(allowed, jnp.exp(scores - jnp.max(scores, axis=-1, keepdims=True)), 0.0)
        totals = jnp.sum(weights, axis=-1, keepdims=True)
        att[k] = (dot(weights.astype(BF16), values) / totals).astype(BF16)
        send(remote(att.at[k], mix.at[c, x], r_send.at[k], r_recv.at[x], (block, c)), block != s)

        @pl.when(block == s)
        def _():
            mix[c, x] = att[k]

    across = seq_at((1, 0))
    arrive(win.at[across], wi_recv.at[0])
    for i in (1, 3, 2):
        send(remote(win.at[across], win.at[across], wi_send.at[3 + i], wi_recv.at[3 + i], (seq_at((0, i)), c)))
    send(remote(win.at[across], win.at[across], wf_send.at[1], wf_recv.at[1], (sibling, c)))

    for g in range(4):
        @pl.when(jnp.logical_or(g != x, owner != rank))
        def _():
            arrive(mix.at[c, g], r_recv.at[g])

    for i, step in enumerate(CB_STEPS):
        send(remote(mix.at[c], mix.at[c], m_send.at[i], m_recv.at[i], (s, cb_at(step))))

    def group_term(group):
        top = jnp.concatenate([mix[group, 0], mix[group, 1]], axis=1)
        low = jnp.concatenate([mix[group, 2], mix[group, 3]], axis=1)
        return dot(jnp.concatenate([top, low], axis=0), wo[group])

    loads[4].wait()
    summed = group_term(c)
    for i, step in enumerate(CB_STEPS):
        group = cb_at(step, -1)
        arrive(wo.at[group], wo_recv.at[i])
        arrive(mix.at[group], m_recv.at[i])
        summed = summed + group_term(group)
    mine = pl.ds(pl.multiple_of(c * 512, 512), 512)
    tb[c] = (hid[:, mine].astype(F32) + summed).astype(BF16)
    for i, step in enumerate(CB_STEPS):
        send(remote(tb.at[c], tb.at[c], t_send.at[i], t_recv.at[i], (s, cb_at(step))))
    stores = []

    def store(index, group):
        columns = pl.ds(pl.multiple_of(group * 512, 512), 512)
        copy = pltpu.make_async_copy(tb.at[group], temporal_out.at[:, columns], to_sem.at[index])
        copy.start()
        stores.append(copy)

    store(7, c)

    loads[6].wait()
    picks = []
    for b in range(2):
        picks.append(jnp.broadcast_to(ids[b : b + 1, :], (128, 128)).T)
    acc[...] = jnp.zeros_like(acc)

    @pl.loop(0, 8)
    def _(k):
        lane = lax.broadcasted_iota(jnp.int32, (128, 128), 1) + k * 256
        hot = [
            jnp.concatenate([jnp.where(pick == lane + 128 * j, 1.0, 0.0).astype(BF16) for j in range(2)], axis=1)
            for pick in picks
        ]
        acc[...] += dot(jnp.concatenate(hot, axis=0), emb[pl.ds(pl.multiple_of(k * 256, 256), 256), :])

    loads[5].wait()
    for i in (1, 3, 2):
        source = seq_at((0, i), -1)
        arrive(win.at[source], wi_recv.at[i])
        send(remote(win.at[source], win.at[source], wf_send.at[1 + i], wf_recv.at[1 + i], (sibling, c)))
    for i in (1, 3, 2):
        source = seq_at((1, i), -1)
        arrive(win.at[source], wi_recv.at[3 + i])
        send(remote(win.at[source], win.at[source], wf_send.at[4 + i], wf_recv.at[4 + i], (sibling, c)))
    twin = 1 - 2 * co
    arrive(win.at[sibling], wf_recv.at[0])
    arrive(win.at[across + twin], wf_recv.at[1])
    for i in (1, 3, 2):
        arrive(win.at[seq_at((0, i), -1) + twin], wf_recv.at[1 + i])
        arrive(win.at[seq_at((1, i), -1) + twin], wf_recv.at[4 + i])

    def add_block(group):
        rows = jnp.concatenate([win[2 * group], win[2 * group + 1]], axis=0)
        acc[...] += dot(tb[group], rows)

    add_block(c)
    for i, step in enumerate(CB_STEPS):
        group = cb_at(step, -1)
        arrive(tb.at[group], t_recv.at[i])
        store(i, group)
        add_block(group)

    @pl.loop(0, 8)
    def _(i):
        rows = pl.ds(pl.multiple_of(i * 32, 32), 32)
        rounded = acc[rows, :].astype(BF16)
        stream[rows, :] = rounded
        values = rounded.astype(F32)
        mean_sq = jnp.mean(values * values, axis=-1, keepdims=True)
        dnorm[rows, :] = (values * lax.rsqrt(mean_sq + EPS) * depth_gain[...]).astype(BF16)

    loads[7].wait()
    for i in (2, 1, 3, 0):
        pair = (c // 2 + i) % 4
        columns = pl.ds(pl.multiple_of(pair * 256, 256), 256)
        for which in range(3):
            res = dot(dnorm[...], dw[which, :, columns]).astype(BF16)
            dsend[2 * pair, which] = res[:, 0:128]
            dsend[2 * pair + 1, which] = res[:, 128:256]
        if i:
            for j in range(2):
                to = 2 * pair + j
                send(remote(dsend.at[to], drecv.at[c], d_send.at[2 * i + j], d_recv.at[c], (s, to)))
        else:
            to = c + 1 - 2 * (c % 2)
            send(remote(dsend.at[to], drecv.at[c], d_send.at[0], d_recv.at[c], (s, to)))
            drecv[c] = dsend[c]

    for book in range(8):
        @pl.when(book != c)
        def _():
            arrive(drecv.at[book], d_recv.at[book])

    half_a = lax.broadcasted_iota(jnp.int32, (256, 128), 0) % 128 // 64
    half_b = lax.broadcasted_iota(jnp.int32, (256, 128), 1) // 64
    same_head = jnp.where(half_a == half_b, 1.0, 0.0).astype(BF16)
    size = 64
    for book in range(8):
        @pl.loop(0, 256 // size)
        def _(i):
            rows = pl.ds(pl.multiple_of(i * size, size), size)
            query = drecv[book, 0, rows, :].astype(F32)
            parts = []
            for j in range(book + 1):
                prod = query * drecv[j, 1, rows, :].astype(F32)
                high = prod.astype(BF16)
                low = (prod - high.astype(F32)).astype(BF16)
                parts.append(jnp.concatenate([high, low], axis=1))
            scores = dot(jnp.concatenate(parts, axis=0), same_head)
            scores = [scores[j * size : (j + 1) * size] for j in range(book + 1)]
            highest = scores[0]
            for j in range(1, book + 1):
                highest = jnp.maximum(highest, scores[j])
            totals = jnp.zeros((size, 128), F32)
            mixed = jnp.zeros((size, 128), F32)
            for j in range(book + 1):
                weight = jnp.exp((scores[j] - highest) * 0.125)
                totals = totals + weight
                mixed = mixed + weight.astype(BF16).astype(F32) * drecv[j, 2, rows, :].astype(F32)
            bsend[book, rows, :] = (mixed / totals).astype(BF16)

        send(remote(bsend.at[book], brecv.at[c], b_send.at[book], b_recv.at[c], (s, book)), book != c)

        @pl.when(book == c)
        def _():
            brecv[c] = bsend[book]

    loads[8].wait()
    for head in range(8):
        @pl.when(head != c)
        def _():
            arrive(brecv.at[head], b_recv.at[head])

    book_mixed = jnp.concatenate([brecv[head] for head in range(8)], axis=1)
    depth_res[...] = (dot(book_mixed, do[...]) + stream[...].astype(F32)).astype(BF16)

    for copy in stores:
        copy.wait()
    for copy, when in pending:
        if when is None:
            copy.wait_send()
        else:
            pl.when(when)(copy.wait_send)


def shards(hidden, gain, qkv_w, out_w, ids, embedding, in_w, depth_gain, depth_qkv, depth_out):
    anywhere = pl.BlockSpec(memory_space=pl.ANY)
    vmem = pl.BlockSpec(memory_space=pltpu.VMEM)
    dma = pltpu.SemaphoreType.DMA
    temporal, depth = pl.pallas_call(
        body,
        out_shape=(jax.ShapeDtypeStruct((256, 4096), BF16), jax.ShapeDtypeStruct((256, 1024), BF16)),
        in_specs=[anywhere, vmem, anywhere, anywhere, vmem, anywhere, anywhere, vmem, anywhere, anywhere],
        out_specs=(anywhere, vmem),
        scratch_shapes=[
            pltpu.VMEM((256, 4096), BF16),
            pltpu.VMEM((256, 4096), BF16),
            pltpu.VMEM((3, 4096, 256), BF16),
            pltpu.VMEM((4, 3, 128, 128), BF16),
            pltpu.VMEM((16, 2, 128, 128), BF16),
            pltpu.VMEM((4, 128, 128), BF16),
            pltpu.VMEM((4, 128, 128), BF16),
            pltpu.VMEM((8, 4, 128, 128), BF16),
            pltpu.VMEM((8, 256, 512), BF16),
            pltpu.VMEM((8, 256, 512), BF16),
            pltpu.VMEM((16, 256, 1024), BF16),
            pltpu.VMEM((2048, 1024), BF16),
            pltpu.VMEM((3, 1024, 1024), BF16),
            pltpu.VMEM((1024, 1024), BF16),
            pltpu.VMEM((256, 1024), F32),
            pltpu.VMEM((256, 1024), BF16),
            pltpu.VMEM((256, 1024), BF16),
            pltpu.VMEM((8, 3, 256, 128), BF16),
            pltpu.VMEM((8, 3, 256, 128), BF16),
            pltpu.VMEM((8, 256, 128), BF16),
            pltpu.VMEM((8, 256, 128), BF16),
            dma((9,)),
            dma((7,)), dma((7,)),
            dma((8,)), dma((8,)),
            dma((4,)), dma((4,)),
            dma((4,)), dma((4,)),
            dma((7,)), dma((7,)),
            dma((7,)), dma((7,)),
            dma((7,)), dma((7,)),
            dma((8,)),
            dma((7,)), dma((7,)),
            dma((8,)), dma((8,)),
            dma((8,)), dma((8,)),
            dma((8,)), dma((8,)),
        ],
        compiler_params=pltpu.CompilerParams(
            collective_id=0, has_side_effects=True, vmem_limit_bytes=60 * 1024 * 1024
        ),
    )(
        hidden.reshape(256, 4096),
        gain.reshape(1, 4096),
        qkv_w,
        out_w,
        ids.reshape(2, 128),
        embedding[0],
        in_w[0],
        depth_gain,
        depth_qkv[0],
        depth_out[0],
    )
    return temporal.reshape(2, 128, 4096), depth.reshape(2, 128, 1, 1024)


def solution(mesh):
    placed = (
        P(None, "seq", None),
        P(),
        P(None, None, "cb"),
        P("cb", None),
        P(None, "seq", "cb"),
        P("cb", None, None),
        P("cb", "seq", None),
        P("cb", None),
        P("cb", None, None, None),
        P("cb", None, None),
    )
    return jax.shard_map(
        shards,
        mesh=mesh,
        in_specs=placed,
        out_specs=(P(None, "seq", None), P(None, "seq", "cb", None)),
        check_vma=False,
    )
```

```python
import jax
import jax.numpy as jnp
from jax import lax
from jax.experimental import pallas as pl
from jax.experimental.pallas import tpu as pltpu
from jax.sharding import PartitionSpec as P

MESH = pl.DeviceIdType.MESH
F32, BF16 = jnp.float32, jnp.bfloat16
EPS = 1e-05
CB_STEPS = [(0, 1), (0, 3), (0, 2), (1, 0), (1, 1), (1, 3), (1, 2)]
SEQ_STEPS = [(0, 1), (0, 3), (1, 0), (0, 2), (1, 1), (1, 3), (1, 2)]


def dot(a, b):
    return jnp.dot(a, b, preferred_element_type=F32)


def body(
    hidden, gain, qkv_w, out_w, ids, embedding, in_w, depth_gain, depth_qkv, depth_out,
    temporal_out, depth_res,
    hid, normed, wq, kvq, kv, qs, att, mix, wo, tb, win, emb, dw, do, acc, stream, dnorm, dsend, drecv, bsend, brecv,
    local_sem, kv_send, kv_recv, kvf_send, kvf_recv, q_send, q_recv, r_send, r_recv, m_send, m_recv,
    wo_send, wo_recv, wof_send, wof_recv, t_send, t_recv, to_sem, wi_send, wi_recv, wf_send, wf_recv, d_send, d_recv, b_send, b_recv,
):
    s = lax.axis_index("seq")
    c = lax.axis_index("cb")
    yl, x, co = s // 8, (s // 2) % 4, s % 2
    yh, z = c // 4, c % 4
    rank = yl * 2 + co

    def cb_at(step, sign=1):
        return ((yh + step[0]) % 2) * 4 + (z + sign * step[1] + 4) % 4

    def seq_at(step, sign=1):
        return ((yl + step[0]) % 2) * 8 + ((x + sign * step[1] + 4) % 4) * 2 + co

    sibling = s + 1 - 2 * co

    def remote(src, dst, send, recv, device):
        return pltpu.make_async_remote_copy(
            src_ref=src, dst_ref=dst, send_sem=send, recv_sem=recv, device_id=device, device_id_type=MESH
        )

    def arrive(ref, sem):
        pltpu.make_async_copy(ref, ref, sem).wait()

    pending = []

    def send(copy, when=None):
        if when is None:
            copy.start()
        else:
            pl.when(when)(copy.start)
        pending.append((copy, when))

    partner = cb_at((1, 0))
    up, down = cb_at((0, 1)), cb_at((0, 3))

    def lane_send(part, b, sems, row, lane, h, block, to):
        sends, recvs = sems
        ref = part(block, b, h)
        index = 13 * b + 1 + 6 * row + lane
        send(remote(ref, ref, sends.at[index], recvs.at[index], (s, to)))

    def lane_arrive(part, b, sems, row, lane):
        step, h = ((3, 0), (3, 1), (1, 0), (1, 1), (2, 0), (2, 1))[lane]
        arrive(part(cb_at((row, step)), b, h), sems[1].at[13 * b + 1 + 6 * row + lane])

    def along(part, b, sems, row):
        block = partner if row else c
        for lane, h, to in ((0, 0, up), (3, 1, down), (1, 1, up), (2, 0, down)):
            lane_send(part, b, sems, row, lane, h, block, to)

    def spread(part, b, sems):
        own = part(c, b, None)
        send(remote(own, own, sems[0].at[13 * b], sems[1].at[13 * b], (s, partner)))
        along(part, b, sems, 0)

    def pass_on(part, b, sems):
        arrive(part(partner, b, None), sems[1].at[13 * b])
        along(part, b, sems, 1)

    def relay(part, b, sems, row):
        lane_arrive(part, b, sems, row, 0)
        lane_send(part, b, sems, row, 4, 0, cb_at((row, 3)), up)
        lane_arrive(part, b, sems, row, 3)
        lane_send(part, b, sems, row, 5, 1, cb_at((row, 1)), down)

    def arrivals(part, b, sems):
        yield partner
        for row in range(2):
            for lane, step in ((1, 3), (2, 1)):
                lane_arrive(part, b, sems, row, lane)
                yield cb_at((row, step))
        for row in range(2):
            for lane in (4, 5):
                lane_arrive(part, b, sems, row, lane)
            yield cb_at((row, 2))

    def forward(part, sems):
        pass_on(part, 0, sems)
        relay(part, 0, sems, 0)
        pass_on(part, 1, sems)
        relay(part, 1, sems, 0)
        relay(part, 0, sems, 1)
        relay(part, 1, sems, 1)

    def mix_part(group, b, h):
        return mix.at[group, pl.ds(2 * b, 2) if h is None else 2 * b + h]

    def tb_part(group, b, h):
        return tb.at[group, pl.ds(128 * b, 128) if h is None else pl.ds(128 * b + 64 * h, 64)]

    mix_sems, tb_sems = (m_send, m_recv), (t_send, t_recv)

    across = seq_at((1, 0))
    right, left = seq_at((0, 1)), seq_at((0, 3))

    def in_half(block, h):
        return win.at[block, pl.ds(128 * h, 128)]

    def in_send(row, lane, ref, source, to):
        send(remote(source, ref, wi_send.at[1 + 6 * row + lane], wi_recv.at[1 + 6 * row + lane], (to, c)))

    def in_arrive(row, lane):
        step, h = ((3, 0), (3, 1), (1, 0), (1, 1), (2, 0), (2, 1))[lane]
        arrive(in_half(seq_at((row, step)), h), wi_recv.at[1 + 6 * row + lane])

    def in_relay(row):
        in_arrive(row, 0)
        ref = in_half(seq_at((row, 3)), 0)
        in_send(row, 4, ref, ref, right)
        in_arrive(row, 3)
        ref = in_half(seq_at((row, 1)), 1)
        in_send(row, 5, ref, ref, left)

    def in_share(block, index):
        send(remote(win.at[block], win.at[block], wf_send.at[index], wf_recv.at[index], (sibling, c)))

    barrier = pltpu.get_barrier_semaphore()
    for step in CB_STEPS:
        pl.semaphore_signal(barrier, inc=1, device_id=(s, cb_at(step)), device_id_type=MESH)
    for step in SEQ_STEPS:
        pl.semaphore_signal(barrier, inc=1, device_id=(seq_at(step), c), device_id_type=MESH)
        other = seq_at(step) + 1 - 2 * co
        pl.semaphore_signal(barrier, inc=1, device_id=(other, c), device_id_type=MESH)
    pl.semaphore_signal(barrier, inc=1, device_id=(sibling, c), device_id_type=MESH)

    loads = [
        pltpu.make_async_copy(hidden, hid, local_sem.at[0]),
        pltpu.make_async_copy(qkv_w.at[1], wq.at[1], local_sem.at[1]),
        pltpu.make_async_copy(qkv_w.at[2], wq.at[2], local_sem.at[2]),
        pltpu.make_async_copy(qkv_w.at[0], wq.at[0], local_sem.at[3]),
        pltpu.make_async_copy(out_w.at[:, pl.ds(pl.multiple_of(c * 512, 512), 512)], wo.at[c], local_sem.at[4]),
        pltpu.make_async_copy(in_w, win.at[s], local_sem.at[5]),
        pltpu.make_async_copy(embedding, emb, local_sem.at[6]),
        pltpu.make_async_copy(depth_qkv, dw, local_sem.at[7]),
        pltpu.make_async_copy(depth_out, do, local_sem.at[8]),
    ]
    for copy in loads:
        copy.start()

    loads[0].wait()

    @pl.loop(0, 16)
    def _(i):
        rows = pl.ds(pl.multiple_of(i * 16, 16), 16)
        values = hid[rows, :].astype(F32)
        mean_sq = jnp.mean(values * values, axis=-1, keepdims=True)
        normed[rows, :] = (values * lax.rsqrt(mean_sq + EPS) * gain[...]).astype(BF16)

    def project(which, slot):
        loads[{1: 1, 2: 2, 0: 3}[which]].wait()
        res = dot(normed[...], wq[which]).astype(BF16)
        for g in range(4):
            b, h = g // 2, g % 2
            kvq[g, slot] = res[b * 128 : (b + 1) * 128, h * 128 : (h + 1) * 128]

    pl.semaphore_wait(barrier, 22)
    half = pl.ds(pl.multiple_of(co * 128, 128), 128)
    for i, step in enumerate(CB_STEPS):
        to = cb_at(step)
        columns = pl.ds(pl.multiple_of(to * 512, 512), 512)
        send(remote(out_w.at[half, columns], wo.at[c, half], wo_send.at[i], wo_recv.at[i], (s, to)))
    in_send(0, 0, in_half(s, 0), in_w.at[pl.ds(0, 128)], right)
    in_send(0, 3, in_half(s, 1), in_w.at[pl.ds(128, 128)], left)

    project(1, 0)
    project(2, 1)

    for i, step in enumerate(SEQ_STEPS):
        to = seq_at(step)
        g = (to // 2) % 4
        send(remote(kvq.at[g, pl.ds(0, 2)], kv.at[s], kv_send.at[i], kv_recv.at[i], (to, c)))
    kv[s] = kvq[x, 0:2]
    send(remote(kv.at[s], kv.at[s], kvf_send.at[7], kvf_recv.at[7], (sibling, c)))

    project(0, 2)
    turn = s % 8
    owner = jnp.where(turn < 4, turn, 7 - turn)
    strip = s // 4
    for dx in range(4):
        g = (x + dx) % 4
        to = (owner // 2) * 8 + g * 2 + owner % 2
        copy = remote(kvq.at[g, 2], qs.at[strip], q_send.at[dx], q_recv.at[strip], (to, c))
        send(copy, None if dx else owner != rank)

    @pl.when(owner == rank)
    def _():
        qs[strip] = kvq[x, 2]

    send(remote(in_w, win.at[s], wi_send.at[0], wi_recv.at[0], (across, c)))
    in_send(0, 1, in_half(s, 1), in_w.at[pl.ds(128, 128)], right)
    in_send(0, 2, in_half(s, 0), in_w.at[pl.ds(0, 128)], left)
    send(remote(in_w, win.at[s], wf_send.at[0], wf_recv.at[0], (sibling, c)))
    in_relay(0)
    for i, step in enumerate(CB_STEPS):
        group = cb_at(step, -1)
        arrive(wo.at[group, half], wo_recv.at[i])
        send(remote(wo.at[group, half], wo.at[group, half], wof_send.at[i], wof_recv.at[i], (sibling, c)))

    for i, step in enumerate(SEQ_STEPS):
        source = seq_at(step, -1)
        arrive(kv.at[source], kv_recv.at[i])
        send(remote(kv.at[source], kv.at[source], kvf_send.at[i], kvf_recv.at[i], (sibling, c)))
    arrive(kv.at[sibling], kvf_recv.at[7])
    for i, step in enumerate(SEQ_STEPS):
        source = seq_at(step, -1) + 1 - 2 * co
        arrive(kv.at[source], kvf_recv.at[i])

    for k in range(4):
        block = 4 * k + (rank if k % 2 == 0 else 3 - rank)

        @pl.when(block != s)
        def _():
            arrive(qs.at[k], q_recv.at[k])

        n = 4 * (k + 1)
        keys = kv[0:n, 0].reshape(n * 128, 128)
        values = kv[0:n, 1].reshape(n * 128, 128)
        scores = lax.dot_general(qs[k], keys, (((1,), (1,)), ((), ())), preferred_element_type=F32)
        row = lax.broadcasted_iota(jnp.int32, scores.shape, 0) + block * 128
        col = lax.broadcasted_iota(jnp.int32, scores.shape, 1)
        allowed = col <= row
        scores = jnp.where(allowed, scores * (128.0**-0.5), -1e30)
        weights = jnp.where(allowed, jnp.exp(scores - jnp.max(scores, axis=-1, keepdims=True)), 0.0)
        totals = jnp.sum(weights, axis=-1, keepdims=True)
        att[k] = (dot(weights.astype(BF16), values) / totals).astype(BF16)
        send(remote(att.at[k], mix.at[c, x], r_send.at[k], r_recv.at[x], (block, c)), block != s)

        @pl.when(block == s)
        def _():
            mix[c, x] = att[k]

    for b in range(2):
        for g in (2 * b, 2 * b + 1):
            @pl.when(jnp.logical_or(g != x, owner != rank))
            def _():
                arrive(mix.at[c, g], r_recv.at[g])

        spread(mix_part, b, mix_sems)

    arrive(win.at[across], wi_recv.at[0])
    for lane, h, to in ((0, 0, right), (3, 1, left), (1, 1, right), (2, 0, left)):
        in_send(1, lane, in_half(across, h), in_half(across, h), to)
    forward(mix_part, mix_sems)

    loads[6].wait()
    picks = []
    for b in range(2):
        picks.append(jnp.broadcast_to(ids[b : b + 1, :], (128, 128)).T)
    acc[...] = jnp.zeros_like(acc)

    @pl.loop(0, 8)
    def _(k):
        lane = lax.broadcasted_iota(jnp.int32, (128, 128), 1) + k * 256
        hot = [
            jnp.concatenate([jnp.where(pick == lane + 128 * j, 1.0, 0.0).astype(BF16) for j in range(2)], axis=1)
            for pick in picks
        ]
        acc[...] += dot(jnp.concatenate(hot, axis=0), emb[pl.ds(pl.multiple_of(k * 256, 256), 256), :])
    loads[5].wait()
    for lane in (1, 2, 4, 5):
        in_arrive(0, lane)
    for i in (1, 3, 2):
        in_share(seq_at((0, i)), 1 + i)

    def group_term(group, b):
        return dot(jnp.concatenate([mix[group, 2 * b], mix[group, 2 * b + 1]], axis=1), wo[group])

    loads[4].wait()
    other_half = pl.ds(pl.multiple_of(128 - co * 128, 128), 128)
    for i, step in enumerate(CB_STEPS):
        arrive(wo.at[cb_at(step, -1), other_half], wof_recv.at[i])
    mine = pl.ds(pl.multiple_of(c * 512, 512), 512)
    for b in range(2):
        summed = group_term(c, b)
        for group in arrivals(mix_part, b, mix_sems):
            summed = summed + group_term(group, b)
        rows = pl.ds(128 * b, 128)
        tb[c, rows, :] = (hid[rows, mine].astype(F32) + summed).astype(BF16)
        spread(tb_part, b, tb_sems)
    stores = []

    def store(index, group):
        columns = pl.ds(pl.multiple_of(group * 512, 512), 512)
        copy = pltpu.make_async_copy(tb.at[group], temporal_out.at[:, columns], to_sem.at[index])
        copy.start()
        stores.append(copy)

    store(7, c)

    in_relay(1)
    in_share(across, 1)
    forward(tb_part, tb_sems)
    for lane in (1, 2, 4, 5):
        in_arrive(1, lane)
    for i in (1, 3, 2):
        in_share(seq_at((1, i)), 4 + i)
    twin = 1 - 2 * co
    arrive(win.at[sibling], wf_recv.at[0])
    arrive(win.at[across + twin], wf_recv.at[1])
    for row in range(2):
        for i in (1, 3, 2):
            arrive(win.at[seq_at((row, i)) + twin], wf_recv.at[1 + 3 * row + i])

    loads[7].wait()
    for b in range(2):
        half_rows = pl.ds(128 * b, 128)

        def add_block(group):
            rows = jnp.concatenate([win[2 * group], win[2 * group + 1]], axis=0)
            acc[half_rows, :] += dot(tb[group, half_rows, :], rows)

        add_block(c)
        for i, group in enumerate(arrivals(tb_part, b, tb_sems)):
            if b:
                store(i, group)
            add_block(group)

        @pl.loop(0, 4)
        def _(i):
            rows = pl.ds(pl.multiple_of(i * 32 + 128 * b, 32), 32)
            rounded = acc[rows, :].astype(BF16)
            stream[rows, :] = rounded
            values = rounded.astype(F32)
            mean_sq = jnp.mean(values * values, axis=-1, keepdims=True)
            dnorm[rows, :] = (values * lax.rsqrt(mean_sq + EPS) * depth_gain[...]).astype(BF16)

        for i in (2, 1, 3, 0):
            pair = (c // 2 + i) % 4
            columns = pl.ds(pl.multiple_of(pair * 256, 256), 256)
            for which in range(3):
                res = dot(dnorm[half_rows, :], dw[which, :, columns]).astype(BF16)
                dsend[b, 2 * pair, which] = res[:, 0:128]
                dsend[b, 2 * pair + 1, which] = res[:, 128:256]
            if i:
                for j in range(2):
                    to = 2 * pair + j
                    send(remote(dsend.at[b, to], drecv.at[b, c], d_send.at[8 * b + 2 * i + j], d_recv.at[8 * b + c], (s, to)))
            else:
                to = c + 1 - 2 * (c % 2)
                send(remote(dsend.at[b, to], drecv.at[b, c], d_send.at[8 * b], d_recv.at[8 * b + c], (s, to)))
                drecv[b, c] = dsend[b, c]

    half_a = lax.broadcasted_iota(jnp.int32, (256, 128), 0) % 128 // 64
    half_b = lax.broadcasted_iota(jnp.int32, (256, 128), 1) // 64
    same_head = jnp.where(half_a == half_b, 1.0, 0.0).astype(BF16)
    size = 64
    for b in range(2):
        for book in range(8):
            @pl.when(book != c)
            def _():
                arrive(drecv.at[b, book], d_recv.at[8 * b + book])

        for book in range(8):
            @pl.loop(0, 128 // size)
            def _(i):
                rows = pl.ds(pl.multiple_of(i * size, size), size)
                query = drecv[b, book, 0, rows, :].astype(F32)
                parts = []
                for j in range(book + 1):
                    prod = query * drecv[b, j, 1, rows, :].astype(F32)
                    high = prod.astype(BF16)
                    low = (prod - high.astype(F32)).astype(BF16)
                    parts.append(jnp.concatenate([high, low], axis=1))
                scores = dot(jnp.concatenate(parts, axis=0), same_head)
                scores = [scores[j * size : (j + 1) * size] for j in range(book + 1)]
                highest = scores[0]
                for j in range(1, book + 1):
                    highest = jnp.maximum(highest, scores[j])
                totals = jnp.zeros((size, 128), F32)
                mixed = jnp.zeros((size, 128), F32)
                for j in range(book + 1):
                    weight = jnp.exp((scores[j] - highest) * 0.125)
                    totals = totals + weight
                    mixed = mixed + weight.astype(BF16).astype(F32) * drecv[b, j, 2, rows, :].astype(F32)
                bsend[b, book, rows, :] = (mixed / totals).astype(BF16)

            send(remote(bsend.at[b, book], brecv.at[b, c], b_send.at[8 * b + book], b_recv.at[8 * b + c], (s, book)), book != c)

            @pl.when(book == c)
            def _():
                brecv[b, c] = bsend[b, book]

    loads[8].wait()
    for b in range(2):
        for head in range(8):
            @pl.when(head != c)
            def _():
                arrive(brecv.at[b, head], b_recv.at[8 * b + head])

        book_mixed = jnp.concatenate([brecv[b, head] for head in range(8)], axis=1)
        rows = pl.ds(128 * b, 128)
        depth_res[rows, :] = (dot(book_mixed, do[...]) + stream[rows, :].astype(F32)).astype(BF16)

    for copy in stores:
        copy.wait()
    for copy, when in pending:
        if when is None:
            copy.wait_send()
        else:
            pl.when(when)(copy.wait_send)


def shards(hidden, gain, qkv_w, out_w, ids, embedding, in_w, depth_gain, depth_qkv, depth_out):
    anywhere = pl.BlockSpec(memory_space=pl.ANY)
    hbm = pl.BlockSpec(memory_space=pltpu.HBM)
    vmem = pl.BlockSpec(memory_space=pltpu.VMEM)
    dma = pltpu.SemaphoreType.DMA
    temporal, depth = pl.pallas_call(
        body,
        out_shape=(jax.ShapeDtypeStruct((256, 4096), BF16), jax.ShapeDtypeStruct((256, 1024), BF16)),
        in_specs=[hbm, vmem, hbm, hbm, vmem, hbm, hbm, vmem, hbm, hbm],
        out_specs=(anywhere, vmem),
        scratch_shapes=[
            pltpu.VMEM((256, 4096), BF16),
            pltpu.VMEM((256, 4096), BF16),
            pltpu.VMEM((3, 4096, 256), BF16),
            pltpu.VMEM((4, 3, 128, 128), BF16),
            pltpu.VMEM((16, 2, 128, 128), BF16),
            pltpu.VMEM((4, 128, 128), BF16),
            pltpu.VMEM((4, 128, 128), BF16),
            pltpu.VMEM((8, 4, 128, 128), BF16),
            pltpu.VMEM((8, 256, 512), BF16),
            pltpu.VMEM((8, 256, 512), BF16),
            pltpu.VMEM((16, 256, 1024), BF16),
            pltpu.VMEM((2048, 1024), BF16),
            pltpu.VMEM((3, 1024, 1024), BF16),
            pltpu.VMEM((1024, 1024), BF16),
            pltpu.VMEM((256, 1024), F32),
            pltpu.VMEM((256, 1024), BF16),
            pltpu.VMEM((256, 1024), BF16),
            pltpu.VMEM((2, 8, 3, 128, 128), BF16),
            pltpu.VMEM((2, 8, 3, 128, 128), BF16),
            pltpu.VMEM((2, 8, 128, 128), BF16),
            pltpu.VMEM((2, 8, 128, 128), BF16),
            dma((9,)),
            dma((7,)), dma((7,)),
            dma((8,)), dma((8,)),
            dma((4,)), dma((4,)),
            dma((4,)), dma((4,)),
            dma((26,)), dma((26,)),
            dma((7,)), dma((7,)),
            dma((7,)), dma((7,)),
            dma((26,)), dma((26,)),
            dma((8,)),
            dma((13,)), dma((13,)),
            dma((8,)), dma((8,)),
            dma((16,)), dma((16,)),
            dma((16,)), dma((16,)),
        ],
        compiler_params=pltpu.CompilerParams(
            collective_id=0, has_side_effects=True, vmem_limit_bytes=48 * 1024 * 1024
        ),
    )(
        hidden.reshape(256, 4096),
        gain.reshape(1, 4096),
        qkv_w,
        out_w,
        ids.reshape(2, 128),
        embedding[0],
        in_w[0],
        depth_gain,
        depth_qkv[0],
        depth_out[0],
    )
    return temporal.reshape(2, 128, 4096), depth.reshape(2, 128, 1, 1024)


def solution(mesh):
    placed = (
        P(None, "seq", None),
        P(),
        P(None, None, "cb"),
        P("cb", None),
        P(None, "seq", "cb"),
        P("cb", None, None),
        P("cb", "seq", None),
        P("cb", None),
        P("cb", None, None, None),
        P("cb", None, None),
    )
    return jax.shard_map(
        shards,
        mesh=mesh,
        in_specs=placed,
        out_specs=(P(None, "seq", None), P(None, "seq", "cb", None)),
        check_vma=False,
    )
```

```python
import jax
import jax.numpy as jnp
from jax import lax
from jax.experimental import pallas as pl
from jax.experimental.pallas import tpu as pltpu
from jax.sharding import PartitionSpec as P

MESH = pl.DeviceIdType.MESH
F32, BF16 = jnp.float32, jnp.bfloat16
EPS = 1e-05
CB_STEPS = [(0, 1), (0, 3), (0, 2), (1, 0), (1, 1), (1, 3), (1, 2)]
SEQ_STEPS = [(0, 1), (0, 3), (1, 0), (0, 2), (1, 1), (1, 3), (1, 2)]


def dot(a, b):
    return jnp.dot(a, b, preferred_element_type=F32)


def body(
    hidden, gain, qkv_w, out_w, ids, embedding, in_w, depth_gain, depth_qkv, depth_out,
    temporal_out, depth_res,
    normed, wq, kvq, kv, qs, att, mix, wo, tb, win, emb, dw, do, acc, stream, dnorm, dsend, drecv, bsend, brecv,
    local_sem, kv_send, kv_recv, kvf_send, kvf_recv, q_send, q_recv, r_send, r_recv, m_send, m_recv,
    wo_send, wo_recv, wof_send, wof_recv, t_send, t_recv, to_sem, wi_send, wi_recv, wf_send, wf_recv, d_send, d_recv, b_send, b_recv,
):
    s = lax.axis_index("seq")
    c = lax.axis_index("cb")
    yl, x, co = s // 8, (s // 2) % 4, s % 2
    yh, z = c // 4, c % 4
    rank = yl * 2 + co

    def cb_at(step, sign=1):
        return ((yh + step[0]) % 2) * 4 + (z + sign * step[1] + 4) % 4

    def seq_at(step, sign=1):
        return ((yl + step[0]) % 2) * 8 + ((x + sign * step[1] + 4) % 4) * 2 + co

    sibling = s + 1 - 2 * co

    def remote(src, dst, send, recv, device):
        return pltpu.make_async_remote_copy(
            src_ref=src, dst_ref=dst, send_sem=send, recv_sem=recv, device_id=device, device_id_type=MESH
        )

    def arrive(ref, sem):
        pltpu.make_async_copy(ref, ref, sem).wait()

    pending = []

    def send(copy, when=None):
        if when is None:
            copy.start()
        else:
            pl.when(when)(copy.start)
        pending.append((copy, when))

    partner = cb_at((1, 0))
    up, down = cb_at((0, 1)), cb_at((0, 3))

    def lane_send(part, b, sems, row, lane, h, block, to):
        sends, recvs = sems
        ref = part(block, b, h)
        index = 13 * b + 1 + 6 * row + lane
        send(remote(ref, ref, sends.at[index], recvs.at[index], (s, to)))

    def lane_arrive(part, b, sems, row, lane):
        step, h = ((3, 0), (3, 1), (1, 0), (1, 1), (2, 0), (2, 1))[lane]
        arrive(part(cb_at((row, step)), b, h), sems[1].at[13 * b + 1 + 6 * row + lane])

    def along(part, b, sems, row):
        block = partner if row else c
        for lane, h, to in ((0, 0, up), (3, 1, down), (1, 1, up), (2, 0, down)):
            lane_send(part, b, sems, row, lane, h, block, to)

    def spread(part, b, sems):
        own = part(c, b, None)
        send(remote(own, own, sems[0].at[13 * b], sems[1].at[13 * b], (s, partner)))
        along(part, b, sems, 0)

    def pass_on(part, b, sems):
        arrive(part(partner, b, None), sems[1].at[13 * b])
        along(part, b, sems, 1)

    def relay(part, b, sems, row):
        lane_arrive(part, b, sems, row, 0)
        lane_send(part, b, sems, row, 4, 0, cb_at((row, 3)), up)
        lane_arrive(part, b, sems, row, 3)
        lane_send(part, b, sems, row, 5, 1, cb_at((row, 1)), down)

    def arrivals(part, b, sems):
        yield partner
        for row in range(2):
            for lane, step in ((1, 3), (2, 1)):
                lane_arrive(part, b, sems, row, lane)
                yield cb_at((row, step))
        for row in range(2):
            for lane in (4, 5):
                lane_arrive(part, b, sems, row, lane)
            yield cb_at((row, 2))

    def forward(part, sems):
        pass_on(part, 0, sems)
        relay(part, 0, sems, 0)
        pass_on(part, 1, sems)
        relay(part, 1, sems, 0)
        relay(part, 0, sems, 1)
        relay(part, 1, sems, 1)

    def mix_part(group, b, h):
        return mix.at[group, pl.ds(2 * b, 2) if h is None else 2 * b + h]

    def tb_part(group, b, h):
        return tb.at[group, pl.ds(128 * b, 128) if h is None else pl.ds(128 * b + 64 * h, 64)]

    mix_sems, tb_sems = (m_send, m_recv), (t_send, t_recv)

    across = seq_at((1, 0))
    right, left = seq_at((0, 1)), seq_at((0, 3))

    def in_half(block, h):
        return win.at[block, pl.ds(128 * h, 128)]

    def in_send(row, lane, ref, source, to):
        send(remote(source, ref, wi_send.at[1 + 6 * row + lane], wi_recv.at[1 + 6 * row + lane], (to, c)))

    def in_arrive(row, lane):
        step, h = ((3, 0), (3, 1), (1, 0), (1, 1), (2, 0), (2, 1))[lane]
        arrive(in_half(seq_at((row, step)), h), wi_recv.at[1 + 6 * row + lane])

    def in_relay(row):
        in_arrive(row, 0)
        ref = in_half(seq_at((row, 3)), 0)
        in_send(row, 4, ref, ref, right)
        in_arrive(row, 3)
        ref = in_half(seq_at((row, 1)), 1)
        in_send(row, 5, ref, ref, left)

    def in_share(block, index):
        send(remote(win.at[block], win.at[block], wf_send.at[index], wf_recv.at[index], (sibling, c)))

    barrier = pltpu.get_barrier_semaphore()
    for step in CB_STEPS:
        pl.semaphore_signal(barrier, inc=1, device_id=(s, cb_at(step)), device_id_type=MESH)
    for step in SEQ_STEPS:
        pl.semaphore_signal(barrier, inc=1, device_id=(seq_at(step), c), device_id_type=MESH)
        other = seq_at(step) + 1 - 2 * co
        pl.semaphore_signal(barrier, inc=1, device_id=(other, c), device_id_type=MESH)
    pl.semaphore_signal(barrier, inc=1, device_id=(sibling, c), device_id_type=MESH)

    loads = [
        pltpu.make_async_copy(in_w, win.at[s], local_sem.at[0]),
        pltpu.make_async_copy(qkv_w.at[1], wq.at[1], local_sem.at[1]),
        pltpu.make_async_copy(qkv_w.at[2], wq.at[2], local_sem.at[2]),
        pltpu.make_async_copy(qkv_w.at[0], wq.at[0], local_sem.at[3]),
        pltpu.make_async_copy(out_w.at[:, pl.ds(pl.multiple_of(c * 512, 512), 512)], wo.at[c], local_sem.at[4]),
        None,
        pltpu.make_async_copy(embedding, emb, local_sem.at[6]),
        pltpu.make_async_copy(depth_qkv, dw, local_sem.at[7]),
        pltpu.make_async_copy(depth_out, do, local_sem.at[8]),
    ]
    for copy in loads:
        if copy is not None:
            copy.start()

    @pl.loop(0, 16)
    def _(i):
        rows = pl.ds(pl.multiple_of(i * 16, 16), 16)
        values = hidden[rows, :].astype(F32)
        mean_sq = jnp.mean(values * values, axis=-1, keepdims=True)
        normed[rows, :] = (values * lax.rsqrt(mean_sq + EPS) * gain[...]).astype(BF16)

    def project(which, slot):
        loads[{1: 1, 2: 2, 0: 3}[which]].wait()
        res = dot(normed[...], wq[which]).astype(BF16)
        for g in range(4):
            b, h = g // 2, g % 2
            kvq[g, slot] = res[b * 128 : (b + 1) * 128, h * 128 : (h + 1) * 128]

    pl.semaphore_wait(barrier, 22)
    half = pl.ds(pl.multiple_of(co * 128, 128), 128)
    for i, step in enumerate(CB_STEPS):
        to = cb_at(step)
        columns = pl.ds(pl.multiple_of(to * 512, 512), 512)
        send(remote(out_w.at[half, columns], wo.at[c, half], wo_send.at[i], wo_recv.at[i], (s, to)))
    in_send(0, 0, in_half(s, 0), in_w.at[pl.ds(0, 128)], right)
    in_send(0, 3, in_half(s, 1), in_w.at[pl.ds(128, 128)], left)

    project(1, 0)
    project(2, 1)

    for i, step in enumerate(SEQ_STEPS):
        to = seq_at(step)
        g = (to // 2) % 4
        send(remote(kvq.at[g, pl.ds(0, 2)], kv.at[s], kv_send.at[i], kv_recv.at[i], (to, c)))
    kv[s] = kvq[x, 0:2]
    send(remote(kv.at[s], kv.at[s], kvf_send.at[7], kvf_recv.at[7], (sibling, c)))

    project(0, 2)
    turn = s % 8
    owner = jnp.where(turn < 4, turn, 7 - turn)
    strip = s // 4
    for dx in range(4):
        g = (x + dx) % 4
        to = (owner // 2) * 8 + g * 2 + owner % 2
        copy = remote(kvq.at[g, 2], qs.at[strip], q_send.at[dx], q_recv.at[strip], (to, c))
        send(copy, None if dx else owner != rank)

    @pl.when(owner == rank)
    def _():
        qs[strip] = kvq[x, 2]

    send(remote(in_w, win.at[s], wi_send.at[0], wi_recv.at[0], (across, c)))
    in_send(0, 1, in_half(s, 1), in_w.at[pl.ds(128, 128)], right)
    in_send(0, 2, in_half(s, 0), in_w.at[pl.ds(0, 128)], left)
    send(remote(in_w, win.at[s], wf_send.at[0], wf_recv.at[0], (sibling, c)))
    in_relay(0)
    for i, step in enumerate(CB_STEPS):
        group = cb_at(step, -1)
        arrive(wo.at[group, half], wo_recv.at[i])
        send(remote(wo.at[group, half], wo.at[group, half], wof_send.at[i], wof_recv.at[i], (sibling, c)))

    loads[6].wait()
    picks = []
    for b in range(2):
        picks.append(jnp.broadcast_to(ids[b : b + 1, :], (128, 128)).T)
    acc[...] = jnp.zeros_like(acc)

    @pl.loop(0, 8)
    def _(k):
        lane = lax.broadcasted_iota(jnp.int32, (128, 128), 1) + k * 256
        hot = [
            jnp.concatenate([jnp.where(pick == lane + 128 * j, 1.0, 0.0).astype(BF16) for j in range(2)], axis=1)
            for pick in picks
        ]
        acc[...] += dot(jnp.concatenate(hot, axis=0), emb[pl.ds(pl.multiple_of(k * 256, 256), 256), :])

    for i, step in enumerate(SEQ_STEPS):
        source = seq_at(step, -1)
        arrive(kv.at[source], kv_recv.at[i])
        send(remote(kv.at[source], kv.at[source], kvf_send.at[i], kvf_recv.at[i], (sibling, c)))
    arrive(kv.at[sibling], kvf_recv.at[7])
    for i, step in enumerate(SEQ_STEPS):
        source = seq_at(step, -1) + 1 - 2 * co
        arrive(kv.at[source], kvf_recv.at[i])

    for k in range(4):
        block = 4 * k + (rank if k % 2 == 0 else 3 - rank)

        @pl.when(block != s)
        def _():
            arrive(qs.at[k], q_recv.at[k])

        n = 4 * (k + 1)
        keys = kv[0:n, 0].reshape(n * 128, 128)
        values = kv[0:n, 1].reshape(n * 128, 128)
        scores = lax.dot_general(qs[k], keys, (((1,), (1,)), ((), ())), preferred_element_type=F32)
        row = lax.broadcasted_iota(jnp.int32, scores.shape, 0) + block * 128
        col = lax.broadcasted_iota(jnp.int32, scores.shape, 1)
        allowed = col <= row
        scores = jnp.where(allowed, scores * (128.0**-0.5), -1e30)
        weights = jnp.where(allowed, jnp.exp(scores - jnp.max(scores, axis=-1, keepdims=True)), 0.0)
        totals = jnp.sum(weights, axis=-1, keepdims=True)
        att[k] = (dot(weights.astype(BF16), values) / totals).astype(BF16)
        send(remote(att.at[k], mix.at[c, x], r_send.at[k], r_recv.at[x], (block, c)), block != s)

        @pl.when(block == s)
        def _():
            mix[c, x] = att[k]

    for b in range(2):
        for g in (2 * b, 2 * b + 1):
            @pl.when(jnp.logical_or(g != x, owner != rank))
            def _():
                arrive(mix.at[c, g], r_recv.at[g])

        spread(mix_part, b, mix_sems)

    arrive(win.at[across], wi_recv.at[0])
    for lane, h, to in ((0, 0, right), (3, 1, left), (1, 1, right), (2, 0, left)):
        in_send(1, lane, in_half(across, h), in_half(across, h), to)
    forward(mix_part, mix_sems)

    loads[0].wait()
    for lane in (1, 2, 4, 5):
        in_arrive(0, lane)
    for i in (1, 3, 2):
        in_share(seq_at((0, i)), 1 + i)

    def group_term(group, b):
        return dot(jnp.concatenate([mix[group, 2 * b], mix[group, 2 * b + 1]], axis=1), wo[group])

    loads[4].wait()
    other_half = pl.ds(pl.multiple_of(128 - co * 128, 128), 128)
    for i, step in enumerate(CB_STEPS):
        arrive(wo.at[cb_at(step, -1), other_half], wof_recv.at[i])
    mine = pl.ds(pl.multiple_of(c * 512, 512), 512)
    for b in range(2):
        summed = group_term(c, b)
        for group in arrivals(mix_part, b, mix_sems):
            summed = summed + group_term(group, b)
        rows = pl.ds(128 * b, 128)
        tb[c, rows, :] = (hidden[rows, mine].astype(F32) + summed).astype(BF16)
        spread(tb_part, b, tb_sems)
    stores = []

    def store(index, group):
        columns = pl.ds(pl.multiple_of(group * 512, 512), 512)
        copy = pltpu.make_async_copy(tb.at[group], temporal_out.at[:, columns], to_sem.at[index])
        copy.start()
        stores.append(copy)

    store(7, c)

    in_relay(1)
    in_share(across, 1)
    pass_on(tb_part, 0, tb_sems)
    relay(tb_part, 0, tb_sems, 0)
    pass_on(tb_part, 1, tb_sems)
    relay(tb_part, 1, tb_sems, 0)
    relay(tb_part, 0, tb_sems, 1)
    for lane in (1, 2, 4, 5):
        in_arrive(1, lane)
    for i in (1, 3, 2):
        in_share(seq_at((1, i)), 4 + i)
    twin = 1 - 2 * co
    arrive(win.at[sibling], wf_recv.at[0])
    arrive(win.at[across + twin], wf_recv.at[1])
    for row in range(2):
        for i in (1, 3, 2):
            arrive(win.at[seq_at((row, i)) + twin], wf_recv.at[1 + 3 * row + i])

    loads[7].wait()
    for b in range(2):
        half_rows = pl.ds(128 * b, 128)

        def add_block(group):
            rows = jnp.concatenate([win[2 * group], win[2 * group + 1]], axis=0)
            acc[half_rows, :] += dot(tb[group, half_rows, :], rows)

        add_block(c)
        for i, group in enumerate(arrivals(tb_part, b, tb_sems)):
            if b:
                store(i, group)
            add_block(group)

        @pl.loop(0, 4)
        def _(i):
            rows = pl.ds(pl.multiple_of(i * 32 + 128 * b, 32), 32)
            rounded = acc[rows, :].astype(BF16)
            stream[rows, :] = rounded
            values = rounded.astype(F32)
            mean_sq = jnp.mean(values * values, axis=-1, keepdims=True)
            dnorm[rows, :] = (values * lax.rsqrt(mean_sq + EPS) * depth_gain[...]).astype(BF16)

        if b == 0:
            relay(tb_part, 1, tb_sems, 1)
        for i in (2, 1, 3, 0):
            pair = (c // 2 + i) % 4
            columns = pl.ds(pl.multiple_of(pair * 256, 256), 256)
            for which in range(3):
                res = dot(dnorm[half_rows, :], dw[which, :, columns]).astype(BF16)
                dsend[b, 2 * pair, which] = res[:, 0:128]
                dsend[b, 2 * pair + 1, which] = res[:, 128:256]
            if i:
                for j in range(2):
                    to = 2 * pair + j
                    send(remote(dsend.at[b, to], drecv.at[b, c], d_send.at[8 * b + 2 * i + j], d_recv.at[8 * b + c], (s, to)))
            else:
                to = c + 1 - 2 * (c % 2)
                send(remote(dsend.at[b, to], drecv.at[b, c], d_send.at[8 * b], d_recv.at[8 * b + c], (s, to)))
                drecv[b, c] = dsend[b, c]

    half_a = lax.broadcasted_iota(jnp.int32, (256, 128), 0) % 128 // 64
    half_b = lax.broadcasted_iota(jnp.int32, (256, 128), 1) // 64
    same_head = jnp.where(half_a == half_b, 1.0, 0.0).astype(BF16)
    size = 64
    for b in range(2):
        for book in range(8):
            @pl.when(book != c)
            def _():
                arrive(drecv.at[b, book], d_recv.at[8 * b + book])

        for book in range(8):
            @pl.loop(0, 128 // size)
            def _(i):
                rows = pl.ds(pl.multiple_of(i * size, size), size)
                query = drecv[b, book, 0, rows, :].astype(F32)
                parts = []
                for j in range(book + 1):
                    prod = query * drecv[b, j, 1, rows, :].astype(F32)
                    high = prod.astype(BF16)
                    low = (prod - high.astype(F32)).astype(BF16)
                    parts.append(jnp.concatenate([high, low], axis=1))
                scores = dot(jnp.concatenate(parts, axis=0), same_head)
                scores = [scores[j * size : (j + 1) * size] for j in range(book + 1)]
                highest = scores[0]
                for j in range(1, book + 1):
                    highest = jnp.maximum(highest, scores[j])
                totals = jnp.zeros((size, 128), F32)
                mixed = jnp.zeros((size, 128), F32)
                for j in range(book + 1):
                    weight = jnp.exp((scores[j] - highest) * 0.125)
                    totals = totals + weight
                    mixed = mixed + weight.astype(BF16).astype(F32) * drecv[b, j, 2, rows, :].astype(F32)
                bsend[b, book, rows, :] = (mixed / totals).astype(BF16)

            send(remote(bsend.at[b, book], brecv.at[b, c], b_send.at[8 * b + book], b_recv.at[8 * b + c], (s, book)), book != c)

            @pl.when(book == c)
            def _():
                brecv[b, c] = bsend[b, book]

    loads[8].wait()
    for b in range(2):
        for head in range(8):
            @pl.when(head != c)
            def _():
                arrive(brecv.at[b, head], b_recv.at[8 * b + head])

        book_mixed = jnp.concatenate([brecv[b, head] for head in range(8)], axis=1)
        rows = pl.ds(128 * b, 128)
        depth_res[rows, :] = (dot(book_mixed, do[...]) + stream[rows, :].astype(F32)).astype(BF16)

    for copy in stores:
        copy.wait()
    for copy, when in pending:
        if when is None:
            copy.wait_send()
        else:
            pl.when(when)(copy.wait_send)


def shards(hidden, gain, qkv_w, out_w, ids, embedding, in_w, depth_gain, depth_qkv, depth_out):
    anywhere = pl.BlockSpec(memory_space=pl.ANY)
    hbm = pl.BlockSpec(memory_space=pltpu.HBM)
    vmem = pl.BlockSpec(memory_space=pltpu.VMEM)
    dma = pltpu.SemaphoreType.DMA
    temporal, depth = pl.pallas_call(
        body,
        out_shape=(jax.ShapeDtypeStruct((256, 4096), BF16), jax.ShapeDtypeStruct((256, 1024), BF16)),
        in_specs=[vmem, vmem, hbm, hbm, vmem, hbm, hbm, vmem, hbm, hbm],
        out_specs=(anywhere, vmem),
        scratch_shapes=[
            pltpu.VMEM((256, 4096), BF16),
            pltpu.VMEM((3, 4096, 256), BF16),
            pltpu.VMEM((4, 3, 128, 128), BF16),
            pltpu.VMEM((16, 2, 128, 128), BF16),
            pltpu.VMEM((4, 128, 128), BF16),
            pltpu.VMEM((4, 128, 128), BF16),
            pltpu.VMEM((8, 4, 128, 128), BF16),
            pltpu.VMEM((8, 256, 512), BF16),
            pltpu.VMEM((8, 256, 512), BF16),
            pltpu.VMEM((16, 256, 1024), BF16),
            pltpu.VMEM((2048, 1024), BF16),
            pltpu.VMEM((3, 1024, 1024), BF16),
            pltpu.VMEM((1024, 1024), BF16),
            pltpu.VMEM((256, 1024), F32),
            pltpu.VMEM((256, 1024), BF16),
            pltpu.VMEM((256, 1024), BF16),
            pltpu.VMEM((2, 8, 3, 128, 128), BF16),
            pltpu.VMEM((2, 8, 3, 128, 128), BF16),
            pltpu.VMEM((2, 8, 128, 128), BF16),
            pltpu.VMEM((2, 8, 128, 128), BF16),
            dma((9,)),
            dma((7,)), dma((7,)),
            dma((8,)), dma((8,)),
            dma((4,)), dma((4,)),
            dma((4,)), dma((4,)),
            dma((26,)), dma((26,)),
            dma((7,)), dma((7,)),
            dma((7,)), dma((7,)),
            dma((26,)), dma((26,)),
            dma((8,)),
            dma((13,)), dma((13,)),
            dma((8,)), dma((8,)),
            dma((16,)), dma((16,)),
            dma((16,)), dma((16,)),
        ],
        compiler_params=pltpu.CompilerParams(
            collective_id=0, has_side_effects=True, vmem_limit_bytes=48 * 1024 * 1024
        ),
    )(
        hidden.reshape(256, 4096),
        gain.reshape(1, 4096),
        qkv_w,
        out_w,
        ids.reshape(2, 128),
        embedding[0],
        in_w[0],
        depth_gain,
        depth_qkv[0],
        depth_out[0],
    )
    return temporal.reshape(2, 128, 4096), depth.reshape(2, 128, 1, 1024)


def solution(mesh):
    placed = (
        P(None, "seq", None),
        P(),
        P(None, None, "cb"),
        P("cb", None),
        P(None, "seq", "cb"),
        P("cb", None, None),
        P("cb", "seq", None),
        P("cb", None),
        P("cb", None, None, None),
        P("cb", None, None),
    )
    return jax.shard_map(
        shards,
        mesh=mesh,
        in_specs=placed,
        out_specs=(P(None, "seq", None), P(None, "seq", "cb", None)),
        check_vma=False,
    )
```
